32 devices in a mesh: row: 8 (over y, x, core), col: 4 (over z).
Axes of the slice: x: 2, y: 2, z: 4, core: 2. Of those that a mesh axis runs over, the one named last changes fastest.
Arguments:
- ancestor_inverse: float32 [6144, 6144], P('row', 'col'), may hold values from -6 to 6
- factor: float32 [6144, 2560], P('row', 'col'), may hold values from -0.078125 to 0.078125
- diag_inverse: float32 [640, 2560], P('row', 'col'), may hold values from -6 to 6
- widths: int32 [4], replicated, may hold values from 384 to 640
- member: int32 [4, 6144], P(None, 'row'), may hold values 0 or 1
Outputs:
- offdiag: float32 [6144, 2560], P('row', 'col')
- diag_blocks: float32 [640, 2560], P('row', 'col')
The draws below stay inside these ranges and needn't reach their ends.
All inputs are finite; a program needn't handle non-finite values. No bound on the sum of `member` on one device may be relied on, other than what follows from the above.
Results may differ from the reference program's by a relative error of at most 0.0001.
Values sent between devices are 32-bit elements; how exact they have to be, the bound alone decides.
A program may use at most 128 MiB of HBM per device.

```python
import jax
import jax.numpy as jnp
from jax import lax

W = 640
NODES = 4
ANC = 6144
COLS = 2560


def place_ends(result, stream_key, least, largest):
    spot = [jax.random.randint(jax.random.fold_in(stream_key, axis), (), 0, length) for axis, length in enumerate(result.shape)]
    widest = result.shape.index(max(result.shape))
    neighbour = spot[:widest] + [(spot[widest] + 1) % result.shape[widest]] + spot[widest + 1:]
    return result.at[tuple(spot)].set(least).at[tuple(neighbour)].set(largest)


def block_scale(stream_key, extent, pieces, least, largest):
    gain, own = 1.0, jax.random.fold_in(stream_key, 6)
    for axis_at, parts in pieces:
        draws = jnp.exp(jax.random.uniform(jax.random.fold_in(own, axis_at), (parts,), jnp.float32, least / len(pieces), largest / len(pieces)))
        gain = gain * jnp.repeat(draws, extent[axis_at] // parts).reshape([-1 if axis == axis_at else 1 for axis in range(len(extent))])
    return gain


def noise(rng, shape, scale, reach, split=(), kind=jnp.bfloat16):
    array = scale * jax.random.normal(rng, shape, jnp.float32)
    if split:
        array = array * block_scale(rng, shape, split, -0.22, 0.18)
    return jnp.clip(array, -reach, reach).astype(kind)


def setup_inputs(seed: int = 0) -> dict:
    seeds = jax.random.split(jax.random.key(seed), 6)
    return {
        "ancestor_inverse": noise(seeds[0], (ANC, ANC), 1.0, 6.0, ((0, 8), (1, 4)), jnp.float32),
        "factor": noise(seeds[1], (ANC, COLS), ANC ** -0.5, 0.078125, ((0, 8), (1, 4)), jnp.float32),
        "diag_inverse": noise(seeds[2], (W, COLS), 1.0, 6.0, ((0, 8), (1, 4)), jnp.float32),
        "widths": place_ends(jax.random.randint(seeds[3], (NODES,), W * 3 // 5, W + 1), jax.random.fold_in(seeds[3], 1), W * 3 // 5, W).astype(jnp.int32),
        "member": place_ends((jax.random.randint(seeds[4], (NODES, ANC), 0, 4) < 3).astype(jnp.int32), jax.random.fold_in(seeds[4], 1), 0, 1),
    }


def reference(ancestor_inverse, factor, diag_inverse, widths, member):
    columns = jnp.arange(NODES * W, dtype=jnp.int32)
    node_of = columns // W
    within = columns % W
    width_col = widths[node_of]
    col_keep = (within < width_col).astype(jnp.float32)
    row_keep = member[node_of].T.astype(jnp.float32)
    mask = row_keep * col_keep[None, :]
    lexp = factor * mask
    product = jnp.dot(ancestor_inverse, lexp, precision=lax.Precision.HIGHEST, preferred_element_type=jnp.float32)
    offdiag = -product * mask
    blocks = []
    for node in range(NODES):
        left = lexp[:, node * W:(node + 1) * W]
        right = product[:, node * W:(node + 1) * W]
        blocks.append(jnp.dot(left.T, right, precision=lax.Precision.HIGHEST, preferred_element_type=jnp.float32))
    gram = jnp.concatenate(blocks, axis=1)
    inside = jnp.arange(W, dtype=jnp.int32)[:, None] < width_col[None, :]
    keep = inside.astype(jnp.float32) * col_keep[None, :]
    diag_blocks = (diag_inverse + gram) * keep
    return offdiag, diag_blocks
```

```python
import functools

import jax
import jax.numpy as jnp
from jax import lax
from jax.experimental import pallas as pl
from jax.experimental.pallas import tpu as pltpu
from jax.sharding import PartitionSpec as P

W = 640
NODES = 4
MESH = pl.DeviceIdType.MESH


def split(x):
    hi = x.astype(jnp.bfloat16)
    lo = (x - hi.astype(jnp.float32)).astype(jnp.bfloat16)
    return hi, lo


def row_tile(rows, most):
    return max(t for t in range(16, most + 1, 16) if rows % t == 0)


def product_kernel(
    R, C, a_ref, l_ref, out_ref, gath, part, recv, a_hi, a_lo, b_hi, b_lo,
    s1, r1, s2, r2, s3, r3, s4, r4,
):
    G = R // C
    half_ring = C // 2
    row = lax.axis_index("row")
    c = lax.axis_index("col")
    j = row // G
    g = lax.rem(row, G)
    rows, cols = l_ref.shape
    chunk = rows // C
    half = rows // 2

    barrier = pltpu.get_barrier_semaphore()

    def greet(r, q):
        pl.semaphore_signal(barrier, inc=1, device_id=(r, q), device_id_type=MESH)

    for n in range(C):
        @pl.when(jnp.logical_or(j != c, j != n))
        def _():
            greet(n * G + g, j)

        @pl.when(jnp.logical_or(j != c, c != n))
        def _():
            greet(c * G + g, n)
    for m in range(1, C):
        greet(lax.rem(j + m, C) * G + g, c)
    for n in range(1, G):
        greet(j * G + lax.rem(g + n, G), c)
    greet(row, lax.rem(c + 1, C))
    greet(row, lax.rem(c + C - 1, C))
    pl.semaphore_wait(barrier, 2 * C + (C - 1) + (G - 1) + 2 - 2 * (j == c).astype(jnp.int32))

    def remote(src, dst, ssem, rsem, r, q):
        return pltpu.make_async_remote_copy(
            src_ref=src, dst_ref=dst, send_sem=ssem, recv_sem=rsem,
            device_id=(r, q), device_id_type=MESH,
        )

    for n in range(C):
        src = l_ref.at[pl.ds(n * chunk, chunk)]
        dst = gath.at[c, g, pl.ds(n * chunk, chunk)]
        own = jnp.logical_and(j == c, j == n)

        @pl.when(jnp.logical_not(own))
        def _():
            remote(src, dst, s1.at[n], r1.at[c], n * G + g, j).start()

        @pl.when(own)
        def _():
            pltpu.make_async_copy(src, dst, r1.at[c]).start()

    ta = row_tile(rows, 128)

    @pl.loop(0, rows // ta)
    def _(t):
        at = pl.ds(pl.multiple_of(t * ta, ta), ta)
        hi, lo = split(a_ref[at, :])
        a_hi[at, :] = hi
        a_lo[at, :] = lo

    order = [(half_ring, 0)]
    for s in range(half_ring - 1, 0, -1):
        order += [(s, -1), (s, 1)]
    order += [(0, 0)]
    blocks = []
    for s, way in order:
        blocks.append(lax.rem(c + (s if way >= 0 else C - s), C))

    mine = pl.ds(pl.multiple_of(j * chunk, chunk), chunk)

    def plane_copy(i, m):
        ref = gath.at[blocks[i], g, mine]
        return remote(ref, ref, s2.at[i, m - 1], r2.at[i, m - 1], lax.rem(j + m, C) * G + g, c)

    def plane_wait(i, m):
        from_j = lax.rem(j + C - m, C)
        ref = gath.at[blocks[i], g, pl.ds(pl.multiple_of(from_j * chunk, chunk), chunk)]
        remote(ref, ref, s2.at[i, m - 1], r2.at[i, m - 1], row, c).wait_recv()

    def group_copy(i, n):
        ref = gath.at[blocks[i], g]
        return remote(ref, ref, s3.at[i, n - 1], r3.at[i, n - 1], j * G + lax.rem(g + n, G), c)

    def group_wait(i, n):
        ref = gath.at[blocks[i], lax.rem(g + G - n, G)]
        remote(ref, ref, s3.at[i, n - 1], r3.at[i, n - 1], row, c).wait_recv()

    for i in range(C):
        q = blocks[i]
        ref = gath.at[q, g, mine]
        remote(ref, ref, s1.at[0], r1.at[q], row, c).wait_recv()
        for m in range(1, C):
            plane_copy(i, m).start()

    tb = row_tile(rows, 128)
    tm = row_tile(rows, 256)

    def multiply(i):
        q = blocks[i]
        for gg in range(G):
            @pl.loop(0, rows // tb)
            def _(t):
                hi, lo = split(gath[q, gg, pl.ds(pl.multiple_of(t * tb, tb), tb), :])
                at = pl.ds(pl.multiple_of(gg * rows + t * tb, tb), tb)
                b_hi[at, :] = hi
                b_lo[at, :] = lo

        @pl.loop(0, rows // tm)
        def _(t):
            at = pl.ds(pl.multiple_of(t * tm, tm), tm)
            dot = functools.partial(jnp.dot, preferred_element_type=jnp.float32)
            x = dot(a_hi[at, :], b_lo[...]) + dot(a_lo[at, :], b_hi[...])
            part[i, at, :] = x + dot(a_hi[at, :], b_hi[...])

    def ring_copy(i, way, s):
        to = lax.rem(c + (C - 1 if way == 0 else 1), C)
        piece = pl.ds(way * half, half) if s == half_ring else pl.ds(0, rows)
        return remote(
            part.at[i, piece], recv.at[way, s - 1, piece],
            s4.at[way, s - 1], r4.at[way, s - 1], row, to,
        )

    def ring_wait(way, s):
        piece = pl.ds(way * half, half) if s + 1 == half_ring else pl.ds(0, rows)
        ref = recv.at[way, s, piece]
        remote(ref, ref, s4.at[way, s], r4.at[way, s], row, c).wait_recv()

    def accumulate(i, way, s):
        lo, n = (way * half, half) if s + 1 == half_ring else (0, rows)
        step = row_tile(n, 128)

        @pl.loop(0, n // step)
        def _(t):
            at = pl.ds(pl.multiple_of(lo + t * step, 16), step)
            part[i, at, :] = part[i, at, :] + recv[way, s, at, :]

    sends = []
    for i, (s, way) in enumerate(order):
        for m in range(1, C):
            plane_wait(i, m)
        for n in range(1, G):
            group_copy(i, n).start()
        for n in range(1, G):
            group_wait(i, n)
        multiply(i)
        if s == half_ring:
            ways = (0, 1)
        elif s:
            ways = (0,) if way < 0 else (1,)
        else:
            ways = ()
        for w in ways:
            if s < half_ring:
                ring_wait(w, s)
                accumulate(i, w, s)
            copy = ring_copy(i, w, s)
            copy.start()
            sends.append(copy)

    ring_wait(0, 0)
    ring_wait(1, 0)

    @pl.loop(0, rows // ta)
    def _(t):
        at = pl.ds(pl.multiple_of(t * ta, ta), ta)
        out_ref[at, :] = part[C - 1, at, :] + recv[0, 0, at, :] + recv[1, 0, at, :]

    for copy in sends:
        copy.wait_send()
    for n in range(C):
        src = l_ref.at[pl.ds(n * chunk, chunk)]

        @pl.when(jnp.logical_or(j != c, j != n))
        def _():
            remote(src, src, s1.at[n], r1.at[0], row, c).wait_send()
    for i in range(C):
        for m in range(1, C):
            plane_copy(i, m).wait_send()
        for n in range(1, G):
            group_copy(i, n).wait_send()


def grid_product(R, C, a, l):
    rows, cols = l.shape
    G = R // C
    depth = a.shape[1]
    vmem = pl.BlockSpec(memory_space=pltpu.VMEM)
    dma = pltpu.SemaphoreType.DMA
    return pl.pallas_call(
        functools.partial(product_kernel, R, C),
        out_shape=jax.ShapeDtypeStruct((rows, cols), jnp.float32),
        in_specs=[vmem, vmem],
        out_specs=vmem,
        scratch_shapes=[
            pltpu.VMEM((C, G, rows, cols), jnp.float32),
            pltpu.VMEM((C, rows, cols), jnp.float32),
            pltpu.VMEM((2, C // 2, rows, cols), jnp.float32),
            pltpu.VMEM((rows, depth), jnp.bfloat16),
            pltpu.VMEM((rows, depth), jnp.bfloat16),
            pltpu.VMEM((depth, cols), jnp.bfloat16),
            pltpu.VMEM((depth, cols), jnp.bfloat16),
            dma((C,)),
            dma((C,)),
            dma((C, C - 1)),
            dma((C, C - 1)),
            dma((C, max(G - 1, 1))),
            dma((C, max(G - 1, 1))),
            dma((2, C // 2)),
            dma((2, C // 2)),
        ],
        compiler_params=pltpu.CompilerParams(
            collective_id=0, has_side_effects=True, vmem_limit_bytes=67043328
        ),
    )(a, l)


def per_device(ancestor_inverse, factor, diag_inverse, widths, member):
    R = lax.axis_size("row")
    C = lax.axis_size("col")
    my_row = lax.axis_index("row")
    my_col = lax.axis_index("col")
    shard_cols = factor.shape[1]
    col_start = my_col * shard_cols
    global_cols = col_start + jnp.arange(shard_cols, dtype=jnp.int32)
    node_of = global_cols // W
    within = global_cols % W
    select = node_of[None, :] == jnp.arange(NODES, dtype=jnp.int32)[:, None]
    width_col = jnp.sum(jnp.where(select, widths[:, None], 0), axis=0)
    col_keep = within < width_col
    pick = jnp.where(select & col_keep[None, :], 1.0, 0.0).astype(jnp.bfloat16)
    mask = lax.dot_general(
        member.astype(jnp.bfloat16), pick, (((0,), (0,)), ((), ())),
        preferred_element_type=jnp.float32,
    )
    masked = factor * mask
    product = grid_product(R, C, ancestor_inverse, masked)
    offdiag = -product * mask
    if shard_cols == W:
        left = masked
    else:
        rows_full = lax.all_gather(masked, "col", axis=1, tiled=True)
        left = lax.dynamic_slice_in_dim(rows_full, col_start // W * W, W, 1)
    local_gram = lax.dot_general(
        left, product, (((0,), (0,)), ((), ())),
        precision=lax.Precision.HIGH, preferred_element_type=jnp.float32,
    )
    gram = lax.psum_scatter(local_gram, "row", scatter_dimension=0, tiled=True)
    diag_rows = diag_inverse.shape[0]
    local_rows = my_row * diag_rows + jnp.arange(diag_rows, dtype=jnp.int32)
    inside = (local_rows[:, None] < width_col[None, :]) & col_keep[None, :]
    diag_blocks = (diag_inverse + gram) * inside.astype(jnp.float32)
    return (offdiag, diag_blocks)


def solution(mesh):
    in_specs = (P("row", "col"), P("row", "col"), P("row", "col"), P(), P(None, "row"))
    out_specs = (P("row", "col"), P("row", "col"))
    return jax.shard_map(
        per_device, mesh=mesh, in_specs=in_specs, out_specs=out_specs, check_vma=False
    )
```

```python
import functools

import jax
import jax.numpy as jnp
from jax import lax
from jax.experimental import pallas as pl
from jax.experimental.pallas import tpu as pltpu
from jax.sharding import PartitionSpec as P

W = 640
NODES = 4
MESH = pl.DeviceIdType.MESH


def split(x):
    hi = x.astype(jnp.bfloat16)
    lo = (x - hi.astype(jnp.float32)).astype(jnp.bfloat16)
    return hi, lo


def row_tile(rows, most):
    return max(t for t in range(16, most + 1, 16) if rows % t == 0)


def product_kernel(
    R, C, a_ref, l_ref, left_ref, out_ref, gram_ref, mid, gath, part, recv, gram, inbox,
    a_hi, a_lo, b_hi, b_lo, s0, r0, s1, r1, s2, r2, s3, r3, s4, r4, s5, r5, own_sem,
):
    G = R // C
    half_ring = C // 2
    row = lax.axis_index("row")
    c = lax.axis_index("col")
    j = row // G
    g = lax.rem(row, G)
    rows, cols = l_ref.shape
    depth = a_ref.shape[1]
    chunk = rows // C
    half = rows // 2

    barrier = pltpu.get_barrier_semaphore()

    def greet(r, q):
        pl.semaphore_signal(barrier, inc=1, device_id=(r, q), device_id_type=MESH)

    for m in range(1, R):
        greet(lax.rem(row + m, R), c)
    for m in range(1, C):
        greet(row, lax.rem(c + m, C))
    pl.semaphore_wait(barrier, R + C - 2)

    def remote(src, dst, ssem, rsem, r, q):
        return pltpu.make_async_remote_copy(
            src_ref=src, dst_ref=dst, send_sem=ssem, recv_sem=rsem,
            device_id=(r, q), device_id_type=MESH,
        )

    mine = pl.ds(pl.multiple_of(j * chunk, chunk), chunk)

    def spread_copy(m):
        n = lax.rem(j + m, C)
        src = l_ref.at[pl.ds(pl.multiple_of(n * chunk, chunk), chunk)]
        return remote(src, mid.at[j], s0.at[m - 1], r0.at[m - 1], n * G + g, c)

    def column_copy(p, m):
        return remote(
            mid.at[p], gath.at[c, g, mine], s1.at[m - 1], r1.at[m - 1], row, p
        )

    for m in range(1, C):
        spread_copy(m).start()
    own = pltpu.make_async_copy(l_ref.at[mine], mid.at[j], own_sem.at[0])
    own.start()
    own.wait()
    for m in range(1, C):
        ref = mid.at[lax.rem(j + C - m, C)]
        remote(ref, ref, s0.at[m - 1], r0.at[m - 1], row, c).wait_recv()
    ways_on = sorted(range(1, C), key=lambda m: -min(m, C - m))
    for m in ways_on:
        column_copy(lax.rem(c + m, C), m).start()
    keep = pltpu.make_async_copy(mid.at[c], gath.at[c, g, mine], own_sem.at[1])
    keep.start()

    ta = row_tile(rows, 128)

    @pl.loop(0, rows // ta)
    def _(t):
        at = pl.ds(pl.multiple_of(t * ta, ta), ta)
        hi, lo = split(a_ref[at, :])
        a_hi[at, pl.ds(0, depth)] = hi
        a_lo[at, pl.ds(0, depth)] = lo

    order = [(half_ring, 0)]
    for s in range(half_ring - 1, 0, -1):
        order += [(s, -1), (s, 1)]
    order += [(0, 0)]
    blocks = []
    for s, way in order:
        blocks.append(lax.rem(c + (s if way >= 0 else C - s), C))

    def plane_copy(i, m):
        ref = gath.at[blocks[i], g, mine]
        return remote(ref, ref, s2.at[i, m - 1], r2.at[i, m - 1], lax.rem(j + m, C) * G + g, c)

    def plane_wait(i, m):
        from_j = lax.rem(j + C - m, C)
        ref = gath.at[blocks[i], g, pl.ds(pl.multiple_of(from_j * chunk, chunk), chunk)]
        remote(ref, ref, s2.at[i, m - 1], r2.at[i, m - 1], row, c).wait_recv()

    def group_copy(i, n):
        ref = gath.at[blocks[i], g]
        return remote(ref, ref, s3.at[i, n - 1], r3.at[i, n - 1], j * G + lax.rem(g + n, G), c)

    def group_wait(i, n):
        ref = gath.at[blocks[i], lax.rem(g + G - n, G)]
        remote(ref, ref, s3.at[i, n - 1], r3.at[i, n - 1], row, c).wait_recv()

    for i, (s, way) in enumerate(order):
        if s:
            m = C - s if way >= 0 else s
            ref = gath.at[blocks[i], g, mine]
            remote(ref, ref, s1.at[m - 1], r1.at[m - 1], row, c).wait_recv()
        else:
            keep.wait()
        for m in range(1, C):
            plane_copy(i, m).start()

    tb = row_tile(rows, 128)
    tm = row_tile(rows, 256)

    def multiply(i):
        q = blocks[i]
        for gg in range(G):
            @pl.loop(0, rows // tb)
            def _(t):
                hi, lo = split(gath[q, gg, pl.ds(pl.multiple_of(t * tb, tb), tb), :])
                at = pl.ds(pl.multiple_of(gg * rows + t * tb, tb), tb)
                b_hi[at, :] = hi
                b_lo[at, :] = lo

        @pl.loop(0, rows // tm)
        def _(t):
            at = pl.ds(pl.multiple_of(t * tm, tm), tm)
            dot = functools.partial(jnp.dot, preferred_element_type=jnp.float32)
            x_hi, x_lo = a_hi[at, pl.ds(0, depth)], a_lo[at, pl.ds(0, depth)]
            y_hi, y_lo = b_hi[pl.ds(0, depth), :], b_lo[pl.ds(0, depth), :]
            part[i, at, :] = dot(x_hi, y_lo) + dot(x_lo, y_hi) + dot(x_hi, y_hi)

    def ring_copy(i, way, s):
        to = lax.rem(c + (C - 1 if way == 0 else 1), C)
        piece = pl.ds(way * half, half) if s == half_ring else pl.ds(0, rows)
        return remote(
            part.at[i, piece], recv.at[way, s - 1, piece],
            s4.at[way, s - 1], r4.at[way, s - 1], row, to,
        )

    def ring_wait(way, s):
        piece = pl.ds(way * half, half) if s + 1 == half_ring else pl.ds(0, rows)
        ref = recv.at[way, s, piece]
        remote(ref, ref, s4.at[way, s], r4.at[way, s], row, c).wait_recv()

    def accumulate(i, way, s):
        lo, n = (way * half, half) if s + 1 == half_ring else (0, rows)
        step = row_tile(n, 128)

        @pl.loop(0, n // step)
        def _(t):
            at = pl.ds(pl.multiple_of(lo + t * step, 16), step)
            part[i, at, :] = part[i, at, :] + recv[way, s, at, :]

    sends = []
    for i, (s, way) in enumerate(order):
        for m in range(1, C):
            plane_wait(i, m)
        for n in range(1, G):
            group_copy(i, n).start()
        for n in range(1, G):
            group_wait(i, n)
        multiply(i)
        if s == half_ring:
            ways = (0, 1)
        elif s:
            ways = (0,) if way < 0 else (1,)
        else:
            ways = ()
        for w in ways:
            if s < half_ring:
                ring_wait(w, s)
                accumulate(i, w, s)
            copy = ring_copy(i, w, s)
            copy.start()
            sends.append(copy)

    ring_wait(0, 0)
    ring_wait(1, 0)

    @pl.loop(0, rows // ta)
    def _(t):
        at = pl.ds(pl.multiple_of(t * ta, ta), ta)
        x = part[C - 1, at, :] + recv[0, 0, at, :] + recv[1, 0, at, :]
        out_ref[at, :] = x
        hi, lo = split(x)
        b_hi[at, :] = hi
        b_lo[at, :] = lo
        hi, lo = split(left_ref[at, :])
        a_hi[at, pl.ds(0, W)] = hi
        a_lo[at, pl.ds(0, W)] = lo

    for t in range(W // 128):
        at = pl.ds(t * 128, 128)
        dot = functools.partial(
            lax.dot_general, dimension_numbers=(((0,), (0,)), ((), ())),
            preferred_element_type=jnp.float32,
        )
        p_hi, p_lo = b_hi[pl.ds(0, rows), :], b_lo[pl.ds(0, rows), :]
        x = dot(a_hi[:, at], p_lo) + dot(a_lo[:, at], p_hi)
        gram[at, :] = x + dot(a_hi[:, at], p_hi)

    share = W // R

    def gram_copy(m):
        to = lax.rem(row + m, R)
        src = gram.at[pl.ds(pl.multiple_of(to * share, 8), share)]
        return remote(src, inbox.at[m - 1], s5.at[m - 1], r5.at[m - 1], to, c)

    for m in range(1, R):
        gram_copy(m).start()
    total = gram[pl.ds(pl.multiple_of(row * share, 8), share), :]
    for m in range(1, R):
        gram_copy(m).wait_recv()
        total = total + inbox[m - 1]
    gram_ref[...] = total

    for copy in sends:
        copy.wait_send()
    for m in range(1, C):
        spread_copy(m).wait_send()
        column_copy(lax.rem(c + m, C), m).wait_send()
    for m in range(1, R):
        gram_copy(m).wait_send()
    for i in range(C):
        for m in range(1, C):
            plane_copy(i, m).wait_send()
        for n in range(1, G):
            group_copy(i, n).wait_send()


def grid_product(R, C, a, l, left):
    rows, cols = l.shape
    G = R // C
    depth = a.shape[1]
    vmem = pl.BlockSpec(memory_space=pltpu.VMEM)
    dma = pltpu.SemaphoreType.DMA
    return pl.pallas_call(
        functools.partial(product_kernel, R, C),
        out_shape=[
            jax.ShapeDtypeStruct((rows, cols), jnp.float32),
            jax.ShapeDtypeStruct((W // R, cols), jnp.float32),
        ],
        in_specs=[vmem, vmem, vmem],
        out_specs=[vmem, vmem],
        scratch_shapes=[
            pltpu.VMEM((C, rows // C, cols), jnp.float32),
            pltpu.VMEM((C, G, rows, cols), jnp.float32),
            pltpu.VMEM((C, rows, cols), jnp.float32),
            pltpu.VMEM((2, C // 2, rows, cols), jnp.float32),
            pltpu.VMEM((W, cols), jnp.float32),
            pltpu.VMEM((R - 1, W // R, cols), jnp.float32),
            pltpu.VMEM((rows, max(depth, W)), jnp.bfloat16),
            pltpu.VMEM((rows, max(depth, W)), jnp.bfloat16),
            pltpu.VMEM((max(depth, rows), cols), jnp.bfloat16),
            pltpu.VMEM((max(depth, rows), cols), jnp.bfloat16),
            dma((C - 1,)),
            dma((C - 1,)),
            dma((C - 1,)),
            dma((C - 1,)),
            dma((C, C - 1)),
            dma((C, C - 1)),
            dma((C, max(G - 1, 1))),
            dma((C, max(G - 1, 1))),
            dma((2, C // 2)),
            dma((2, C // 2)),
            dma((R - 1,)),
            dma((R - 1,)),
            dma((2,)),
        ],
        compiler_params=pltpu.CompilerParams(
            collective_id=0, has_side_effects=True, vmem_limit_bytes=67043328
        ),
    )(a, l, left)


def per_device(ancestor_inverse, factor, diag_inverse, widths, member):
    R = lax.axis_size("row")
    C = lax.axis_size("col")
    my_row = lax.axis_index("row")
    my_col = lax.axis_index("col")
    shard_cols = factor.shape[1]
    col_start = my_col * shard_cols
    global_cols = col_start + jnp.arange(shard_cols, dtype=jnp.int32)
    node_of = global_cols // W
    within = global_cols % W
    select = node_of[None, :] == jnp.arange(NODES, dtype=jnp.int32)[:, None]
    width_col = jnp.sum(jnp.where(select, widths[:, None], 0), axis=0)
    col_keep = within < width_col
    pick = jnp.where(select & col_keep[None, :], 1.0, 0.0).astype(jnp.bfloat16)
    mask = lax.dot_general(
        member.astype(jnp.bfloat16), pick, (((0,), (0,)), ((), ())),
        preferred_element_type=jnp.float32,
    )
    masked = factor * mask
    if shard_cols == W:
        left = masked
    else:
        rows_full = lax.all_gather(masked, "col", axis=1, tiled=True)
        left = lax.dynamic_slice_in_dim(rows_full, col_start // W * W, W, 1)
    product, gram = grid_product(R, C, ancestor_inverse, masked, left)
    offdiag = -product * mask
    diag_rows = diag_inverse.shape[0]
    local_rows = my_row * diag_rows + jnp.arange(diag_rows, dtype=jnp.int32)
    inside = (local_rows[:, None] < width_col[None, :]) & col_keep[None, :]
    diag_blocks = (diag_inverse + gram) * inside.astype(jnp.float32)
    return (offdiag, diag_blocks)


def solution(mesh):
    in_specs = (P("row", "col"), P("row", "col"), P("row", "col"), P(), P(None, "row"))
    out_specs = (P("row", "col"), P("row", "col"))
    return jax.shard_map(
        per_device, mesh=mesh, in_specs=in_specs, out_specs=out_specs, check_vma=False
    )
```

```python
import functools

import jax
import jax.numpy as jnp
from jax import lax
from jax.experimental import pallas as pl
from jax.experimental.pallas import tpu as pltpu
from jax.sharding import PartitionSpec as P

W = 640
NODES = 4
MESH = pl.DeviceIdType.MESH


def split(x):
    hi = x.astype(jnp.bfloat16)
    lo = (x - hi.astype(jnp.float32)).astype(jnp.bfloat16)
    return hi, lo


def row_tile(rows, most):
    return max(t for t in range(16, most + 1, 16) if rows % t == 0)


def product_kernel(
    R, C, a_ref, l_ref, left_ref, out_ref, gram_ref, mid, gath, part, recv, gram, inbox,
    a_hi, a_lo, b_hi, b_lo, s0, r0, s1, r1, s2, r2, s3, r3, s4, r4, s5, r5, own_sem,
):
    G = R // C
    half_ring = C // 2
    row = lax.axis_index("row")
    c = lax.axis_index("col")
    j = row // G
    g = lax.rem(row, G)
    rows, cols = l_ref.shape
    depth = a_ref.shape[1]
    chunk = rows // C
    half = rows // 2

    barrier = pltpu.get_barrier_semaphore()

    def greet(r, q):
        pl.semaphore_signal(barrier, inc=1, device_id=(r, q), device_id_type=MESH)

    for m in range(1, R):
        greet(lax.rem(row + m, R), c)
    for m in range(1, C):
        greet(row, lax.rem(c + m, C))
    pl.semaphore_wait(barrier, R + C - 2)

    def remote(src, dst, ssem, rsem, r, q):
        return pltpu.make_async_remote_copy(
            src_ref=src, dst_ref=dst, send_sem=ssem, recv_sem=rsem,
            device_id=(r, q), device_id_type=MESH,
        )

    mine = pl.ds(pl.multiple_of(j * chunk, chunk), chunk)

    def spread_copy(m):
        n = lax.rem(j + m, C)
        src = l_ref.at[pl.ds(pl.multiple_of(n * chunk, chunk), chunk)]
        return remote(src, mid.at[j], s0.at[m - 1], r0.at[m - 1], n * G + g, c)

    def column_copy(p, m):
        return remote(
            mid.at[p], gath.at[c, g, mine], s1.at[m - 1], r1.at[m - 1], row, p
        )

    for m in range(1, C):
        spread_copy(m).start()
    own = pltpu.make_async_copy(l_ref.at[mine], mid.at[j], own_sem.at[0])
    own.start()
    own.wait()
    for m in range(1, C):
        ref = mid.at[lax.rem(j + C - m, C)]
        remote(ref, ref, s0.at[m - 1], r0.at[m - 1], row, c).wait_recv()
    ways_on = sorted(range(1, C), key=lambda m: -min(m, C - m))
    for m in ways_on:
        column_copy(lax.rem(c + m, C), m).start()
    keep = pltpu.make_async_copy(mid.at[c], gath.at[c, g, mine], own_sem.at[1])
    keep.start()

    ta = row_tile(rows, 128)

    @pl.loop(0, rows // ta)
    def _(t):
        at = pl.ds(pl.multiple_of(t * ta, ta), ta)
        hi, lo = split(a_ref[at, :])
        a_hi[at, pl.ds(0, depth)] = hi
        a_lo[at, pl.ds(0, depth)] = lo

    order = [(half_ring, 0)]
    for s in range(half_ring - 1, 0, -1):
        order += [(s, -1), (s, 1)]
    order += [(0, 0)]
    blocks = []
    for s, way in order:
        blocks.append(lax.rem(c + (s if way >= 0 else C - s), C))

    relay = C == 4
    near = (j + 1 - 2 * lax.rem(j, 2), lax.rem(j + 2, 4))
    part_rows = chunk // 2

    def place(m):
        return lax.rem(j + m, C)

    def source(m):
        return lax.rem(j + C - m, C)

    def piece_copy(i, k, owner, start, size, to):
        at = pl.ds(pl.multiple_of(owner * chunk + start, 8), size)
        ref = gath.at[blocks[i], g, at]
        return remote(ref, ref, s2.at[i, k], r2.at[i, k], to * G + g, c)

    def direct(i):
        if relay:
            return [piece_copy(i, k, j, 0, chunk, near[k]) for k in (0, 1)]
        return [piece_copy(i, m - 1, j, 0, chunk, place(m)) for m in range(1, C)]

    def direct_in(i):
        if relay:
            return [piece_copy(i, k, near[k], 0, chunk, j) for k in (0, 1)]
        return [piece_copy(i, m - 1, source(m), 0, chunk, j) for m in range(1, C)]

    def forward(i, k):
        return piece_copy(i, 2 + k, near[k], k * part_rows, part_rows, near[1 - k])

    def forward_in(i, k):
        far = 3 - j
        return piece_copy(i, 2 + k, far, k * part_rows, part_rows, j)

    def group_copy(i, n):
        ref = gath.at[blocks[i], g]
        return remote(ref, ref, s3.at[i, n - 1], r3.at[i, n - 1], j * G + lax.rem(g + n, G), c)

    def group_wait(i, n):
        ref = gath.at[blocks[i], lax.rem(g + G - n, G)]
        remote(ref, ref, s3.at[i, n - 1], r3.at[i, n - 1], row, c).wait_recv()

    def start_plane(i):
        s, way = order[i]
        if s:
            m = C - s if way >= 0 else s
            ref = gath.at[blocks[i], g, mine]
            remote(ref, ref, s1.at[m - 1], r1.at[m - 1], row, c).wait_recv()
        else:
            keep.wait()
        for copy in direct(i):
            copy.start()

    start_plane(0)
    start_plane(1)

    tb = row_tile(rows, 128)
    tm = row_tile(rows, 256)

    def multiply(i):
        q = blocks[i]
        for gg in range(G):
            @pl.loop(0, rows // tb)
            def _(t):
                hi, lo = split(gath[q, gg, pl.ds(pl.multiple_of(t * tb, tb), tb), :])
                at = pl.ds(pl.multiple_of(gg * rows + t * tb, tb), tb)
                b_hi[at, :] = hi
                b_lo[at, :] = lo

        @pl.loop(0, rows // tm)
        def _(t):
            at = pl.ds(pl.multiple_of(t * tm, tm), tm)
            dot = functools.partial(jnp.dot, preferred_element_type=jnp.float32)
            x_hi, x_lo = a_hi[at, pl.ds(0, depth)], a_lo[at, pl.ds(0, depth)]
            y_hi, y_lo = b_hi[pl.ds(0, depth), :], b_lo[pl.ds(0, depth), :]
            part[i, at, :] = dot(x_hi, y_lo) + dot(x_lo, y_hi) + dot(x_hi, y_hi)

    def ring_copy(i, way, s):
        to = lax.rem(c + (C - 1 if way == 0 else 1), C)
        piece = pl.ds(way * half, half) if s == half_ring else pl.ds(0, rows)
        return remote(
            part.at[i, piece], recv.at[way, s - 1, piece],
            s4.at[way, s - 1], r4.at[way, s - 1], row, to,
        )

    def ring_wait(way, s):
        piece = pl.ds(way * half, half) if s + 1 == half_ring else pl.ds(0, rows)
        ref = recv.at[way, s, piece]
        remote(ref, ref, s4.at[way, s], r4.at[way, s], row, c).wait_recv()

    def accumulate(i, way, s):
        lo, n = (way * half, half) if s + 1 == half_ring else (0, rows)
        step = row_tile(n, 128)

        @pl.loop(0, n // step)
        def _(t):
            at = pl.ds(pl.multiple_of(lo + t * step, 16), step)
            part[i, at, :] = part[i, at, :] + recv[way, s, at, :]

    sends = []
    for i, (s, way) in enumerate(order):
        for k, copy in enumerate(direct_in(i)):
            copy.wait_recv()
            if relay:
                forward(i, k).start()
        if i + 2 < C:
            start_plane(i + 2)
        if relay:
            for k in (0, 1):
                forward_in(i, k).wait_recv()
        for n in range(1, G):
            group_copy(i, n).start()
        for n in range(1, G):
            group_wait(i, n)
        multiply(i)
        if s == half_ring:
            ways = (0, 1)
        elif s:
            ways = (0,) if way < 0 else (1,)
        else:
            ways = ()
        for w in ways:
            if s < half_ring:
                ring_wait(w, s)
                accumulate(i, w, s)
            copy = ring_copy(i, w, s)
            copy.start()
            sends.append(copy)

    ring_wait(0, 0)
    ring_wait(1, 0)

    @pl.loop(0, rows // ta)
    def _(t):
        at = pl.ds(pl.multiple_of(t * ta, ta), ta)
        x = part[C - 1, at, :] + recv[0, 0, at, :] + recv[1, 0, at, :]
        out_ref[at, :] = x
        hi, lo = split(x)
        b_hi[at, :] = hi
        b_lo[at, :] = lo
        hi, lo = split(left_ref[at, :])
        a_hi[at, pl.ds(0, W)] = hi
        a_lo[at, pl.ds(0, W)] = lo

    for t in range(W // 128):
        at = pl.ds(t * 128, 128)
        dot = functools.partial(
            lax.dot_general, dimension_numbers=(((0,), (0,)), ((), ())),
            preferred_element_type=jnp.float32,
        )
        p_hi, p_lo = b_hi[pl.ds(0, rows), :], b_lo[pl.ds(0, rows), :]
        x = dot(a_hi[:, at], p_lo) + dot(a_lo[:, at], p_hi)
        gram[at, :] = x + dot(a_hi[:, at], p_hi)

    share = W // R

    def gram_copy(m):
        to = lax.rem(row + m, R)
        src = gram.at[pl.ds(pl.multiple_of(to * share, 8), share)]
        return remote(src, inbox.at[m - 1], s5.at[m - 1], r5.at[m - 1], to, c)

    for m in range(1, R):
        gram_copy(m).start()
    total = gram[pl.ds(pl.multiple_of(row * share, 8), share), :]
    for m in range(1, R):
        gram_copy(m).wait_recv()
        total = total + inbox[m - 1]
    gram_ref[...] = total

    for copy in sends:
        copy.wait_send()
    for m in range(1, C):
        spread_copy(m).wait_send()
        column_copy(lax.rem(c + m, C), m).wait_send()
    for m in range(1, R):
        gram_copy(m).wait_send()
    for i in range(C):
        for copy in direct(i) + ([forward(i, 0), forward(i, 1)] if relay else []):
            copy.wait_send()
        for n in range(1, G):
            group_copy(i, n).wait_send()


def grid_product(R, C, a, l, left):
    rows, cols = l.shape
    G = R // C
    depth = a.shape[1]
    vmem = pl.BlockSpec(memory_space=pltpu.VMEM)
    dma = pltpu.SemaphoreType.DMA
    return pl.pallas_call(
        functools.partial(product_kernel, R, C),
        out_shape=[
            jax.ShapeDtypeStruct((rows, cols), jnp.float32),
            jax.ShapeDtypeStruct((W // R, cols), jnp.float32),
        ],
        in_specs=[vmem, vmem, vmem],
        out_specs=[vmem, vmem],
        scratch_shapes=[
            pltpu.VMEM((C, rows // C, cols), jnp.float32),
            pltpu.VMEM((C, G, rows, cols), jnp.float32),
            pltpu.VMEM((C, rows, cols), jnp.float32),
            pltpu.VMEM((2, C // 2, rows, cols), jnp.float32),
            pltpu.VMEM((W, cols), jnp.float32),
            pltpu.VMEM((R - 1, W // R, cols), jnp.float32),
            pltpu.VMEM((rows, max(depth, W)), jnp.bfloat16),
            pltpu.VMEM((rows, max(depth, W)), jnp.bfloat16),
            pltpu.VMEM((max(depth, rows), cols), jnp.bfloat16),
            pltpu.VMEM((max(depth, rows), cols), jnp.bfloat16),
            dma((C - 1,)),
            dma((C - 1,)),
            dma((C - 1,)),
            dma((C - 1,)),
            dma((C, C)),
            dma((C, C)),
            dma((C, max(G - 1, 1))),
            dma((C, max(G - 1, 1))),
            dma((2, C // 2)),
            dma((2, C // 2)),
            dma((R - 1,)),
            dma((R - 1,)),
            dma((2,)),
        ],
        compiler_params=pltpu.CompilerParams(
            collective_id=0, has_side_effects=True, vmem_limit_bytes=67043328
        ),
    )(a, l, left)


def per_device(ancestor_inverse, factor, diag_inverse, widths, member):
    R = lax.axis_size("row")
    C = lax.axis_size("col")
    my_row = lax.axis_index("row")
    my_col = lax.axis_index("col")
    shard_cols = factor.shape[1]
    col_start = my_col * shard_cols
    global_cols = col_start + jnp.arange(shard_cols, dtype=jnp.int32)
    node_of = global_cols // W
    within = global_cols % W
    select = node_of[None, :] == jnp.arange(NODES, dtype=jnp.int32)[:, None]
    width_col = jnp.sum(jnp.where(select, widths[:, None], 0), axis=0)
    col_keep = within < width_col
    pick = jnp.where(select & col_keep[None, :], 1.0, 0.0).astype(jnp.bfloat16)
    mask = lax.dot_general(
        member.astype(jnp.bfloat16), pick, (((0,), (0,)), ((), ())),
        preferred_element_type=jnp.float32,
    )
    masked = factor * mask
    if shard_cols == W:
        left = masked
    else:
        rows_full = lax.all_gather(masked, "col", axis=1, tiled=True)
        left = lax.dynamic_slice_in_dim(rows_full, col_start // W * W, W, 1)
    product, gram = grid_product(R, C, ancestor_inverse, masked, left)
    offdiag = -product * mask
    diag_rows = diag_inverse.shape[0]
    local_rows = my_row * diag_rows + jnp.arange(diag_rows, dtype=jnp.int32)
    inside = (local_rows[:, None] < width_col[None, :]) & col_keep[None, :]
    diag_blocks = (diag_inverse + gram) * inside.astype(jnp.float32)
    return (offdiag, diag_blocks)


def solution(mesh):
    in_specs = (P("row", "col"), P("row", "col"), P("row", "col"), P(), P(None, "row"))
    out_specs = (P("row", "col"), P("row", "col"))
    return jax.shard_map(
        per_device, mesh=mesh, in_specs=in_specs, out_specs=out_specs, check_vma=False
    )
```

```python
import functools

import jax
import jax.numpy as jnp
from jax import lax
from jax.experimental import pallas as pl
from jax.experimental.pallas import tpu as pltpu
from jax.sharding import PartitionSpec as P

W = 640
NODES = 4
MESH = pl.DeviceIdType.MESH


def split(x):
    hi = x.astype(jnp.bfloat16)
    lo = (x - hi.astype(jnp.float32)).astype(jnp.bfloat16)
    return hi, lo


def row_tile(rows, most):
    return max(t for t in range(16, most + 1, 16) if rows % t == 0)


def product_kernel(
    R, C, a_ref, l_ref, left_ref, out_ref, gram_ref, mid, gath, part, recv, gram, inbox,
    a_hi, a_lo, b_hi, b_lo, s0, r0, s1, r1, s2, r2, s3, r3, s4, r4, s5, r5, own_sem,
):
    G = R // C
    half_ring = C // 2
    row = lax.axis_index("row")
    c = lax.axis_index("col")
    j = row // G
    g = lax.rem(row, G)
    rows, cols = l_ref.shape
    depth = a_ref.shape[1]
    chunk = rows // C
    half = rows // 2

    barrier = pltpu.get_barrier_semaphore()

    def greet(r, q):
        pl.semaphore_signal(barrier, inc=1, device_id=(r, q), device_id_type=MESH)

    for m in range(1, R):
        greet(lax.rem(row + m, R), c)
    for m in range(1, C):
        greet(row, lax.rem(c + m, C))
    pl.semaphore_wait(barrier, R + C - 2)

    def remote(src, dst, ssem, rsem, r, q):
        return pltpu.make_async_remote_copy(
            src_ref=src, dst_ref=dst, send_sem=ssem, recv_sem=rsem,
            device_id=(r, q), device_id_type=MESH,
        )

    mine = pl.ds(pl.multiple_of(j * chunk, chunk), chunk)

    def spread_copy(m):
        n = lax.rem(j + m, C)
        src = l_ref.at[pl.ds(pl.multiple_of(n * chunk, chunk), chunk)]
        return remote(src, mid.at[j], s0.at[m - 1], r0.at[m - 1], n * G + g, c)

    def column_copy(p, m):
        return remote(
            mid.at[p], gath.at[c, g, mine], s1.at[m - 1], r1.at[m - 1], row, p
        )

    for m in range(1, C):
        spread_copy(m).start()
    own = pltpu.make_async_copy(l_ref.at[mine], mid.at[j], own_sem.at[0])
    own.start()
    own.wait()
    for m in range(1, C):
        ref = mid.at[lax.rem(j + C - m, C)]
        remote(ref, ref, s0.at[m - 1], r0.at[m - 1], row, c).wait_recv()
    ways_on = sorted(range(1, C), key=lambda m: -min(m, C - m))
    for m in ways_on:
        column_copy(lax.rem(c + m, C), m).start()
    keep = pltpu.make_async_copy(mid.at[c], gath.at[c, g, mine], own_sem.at[1])
    keep.start()

    ta = row_tile(rows, 128)

    @pl.loop(0, rows // ta)
    def _(t):
        at = pl.ds(pl.multiple_of(t * ta, ta), ta)
        hi, lo = split(a_ref[at, :])
        a_hi[at, pl.ds(0, depth)] = hi
        a_lo[at, pl.ds(0, depth)] = lo

    order = [(0, 0), (half_ring, 0)]
    for s in range(half_ring - 1, 0, -1):
        order += [(s, -1), (s, 1)]
    blocks = []
    for s, way in order:
        blocks.append(lax.rem(c + (s if way >= 0 else C - s), C))

    def plane_copy(i, m):
        ref = gath.at[blocks[i], g, mine]
        return remote(ref, ref, s2.at[i, m - 1], r2.at[i, m - 1], lax.rem(j + m, C) * G + g, c)

    def plane_wait(i, m):
        from_j = lax.rem(j + C - m, C)
        ref = gath.at[blocks[i], g, pl.ds(pl.multiple_of(from_j * chunk, chunk), chunk)]
        remote(ref, ref, s2.at[i, m - 1], r2.at[i, m - 1], row, c).wait_recv()

    def group_copy(i, n):
        ref = gath.at[blocks[i], g]
        return remote(ref, ref, s3.at[i, n - 1], r3.at[i, n - 1], j * G + lax.rem(g + n, G), c)

    def group_wait(i, n):
        ref = gath.at[blocks[i], lax.rem(g + G - n, G)]
        remote(ref, ref, s3.at[i, n - 1], r3.at[i, n - 1], row, c).wait_recv()

    for i, (s, way) in enumerate(order):
        if s:
            m = C - s if way >= 0 else s
            ref = gath.at[blocks[i], g, mine]
            remote(ref, ref, s1.at[m - 1], r1.at[m - 1], row, c).wait_recv()
        else:
            keep.wait()
        for m in range(1, C):
            plane_copy(i, m).start()

    tb = row_tile(rows, 128)
    tm = row_tile(rows, 256)

    def multiply(i):
        q = blocks[i]
        for gg in range(G):
            @pl.loop(0, rows // tb)
            def _(t):
                hi, lo = split(gath[q, gg, pl.ds(pl.multiple_of(t * tb, tb), tb), :])
                at = pl.ds(pl.multiple_of(gg * rows + t * tb, tb), tb)
                b_hi[at, :] = hi
                b_lo[at, :] = lo

        @pl.loop(0, rows // tm)
        def _(t):
            at = pl.ds(pl.multiple_of(t * tm, tm), tm)
            dot = functools.partial(jnp.dot, preferred_element_type=jnp.float32)
            x_hi, x_lo = a_hi[at, pl.ds(0, depth)], a_lo[at, pl.ds(0, depth)]
            y_hi, y_lo = b_hi[pl.ds(0, depth), :], b_lo[pl.ds(0, depth), :]
            part[i, at, :] = dot(x_hi, y_lo) + dot(x_lo, y_hi) + dot(x_hi, y_hi)

    def ring_copy(i, way, s):
        to = lax.rem(c + (C - 1 if way == 0 else 1), C)
        piece = pl.ds(way * half, half) if s == half_ring else pl.ds(0, rows)
        return remote(
            part.at[i, piece], recv.at[way, s - 1, piece],
            s4.at[way, s - 1], r4.at[way, s - 1], row, to,
        )

    def ring_wait(way, s):
        piece = pl.ds(way * half, half) if s + 1 == half_ring else pl.ds(0, rows)
        ref = recv.at[way, s, piece]
        remote(ref, ref, s4.at[way, s], r4.at[way, s], row, c).wait_recv()

    def accumulate(i, way, s):
        lo, n = (way * half, half) if s + 1 == half_ring else (0, rows)
        step = row_tile(n, 128)

        @pl.loop(0, n // step)
        def _(t):
            at = pl.ds(pl.multiple_of(lo + t * step, 16), step)
            part[i, at, :] = part[i, at, :] + recv[way, s, at, :]

    sends = []
    for i, (s, way) in enumerate(order):
        for m in range(1, C):
            plane_wait(i, m)
        for n in range(1, G):
            group_copy(i, n).start()
        for n in range(1, G):
            group_wait(i, n)
        multiply(i)
        if s == half_ring:
            ways = (0, 1)
        elif s:
            ways = (0,) if way < 0 else (1,)
        else:
            ways = ()
        for w in ways:
            if s < half_ring:
                ring_wait(w, s)
                accumulate(i, w, s)
            copy = ring_copy(i, w, s)
            copy.start()
            sends.append(copy)

    ring_wait(0, 0)
    ring_wait(1, 0)

    @pl.loop(0, rows // ta)
    def _(t):
        at = pl.ds(pl.multiple_of(t * ta, ta), ta)
        x = part[0, at, :] + recv[0, 0, at, :] + recv[1, 0, at, :]
        out_ref[at, :] = x
        hi, lo = split(x)
        b_hi[at, :] = hi
        b_lo[at, :] = lo
        hi, lo = split(left_ref[at, :])
        a_hi[at, pl.ds(0, W)] = hi
        a_lo[at, pl.ds(0, W)] = lo

    for t in range(W // 128):
        at = pl.ds(t * 128, 128)
        dot = functools.partial(
            lax.dot_general, dimension_numbers=(((0,), (0,)), ((), ())),
            preferred_element_type=jnp.float32,
        )
        p_hi, p_lo = b_hi[pl.ds(0, rows), :], b_lo[pl.ds(0, rows), :]
        x = dot(a_hi[:, at], p_lo) + dot(a_lo[:, at], p_hi)
        gram[at, :] = x + dot(a_hi[:, at], p_hi)

    share = W // R

    def gram_copy(m):
        to = lax.rem(row + m, R)
        src = gram.at[pl.ds(pl.multiple_of(to * share, 8), share)]
        return remote(src, inbox.at[m - 1], s5.at[m - 1], r5.at[m - 1], to, c)

    for m in range(1, R):
        gram_copy(m).start()
    total = gram[pl.ds(pl.multiple_of(row * share, 8), share), :]
    for m in range(1, R):
        gram_copy(m).wait_recv()
        total = total + inbox[m - 1]
    gram_ref[...] = total

    for copy in sends:
        copy.wait_send()
    for m in range(1, C):
        spread_copy(m).wait_send()
        column_copy(lax.rem(c + m, C), m).wait_send()
    for m in range(1, R):
        gram_copy(m).wait_send()
    for i in range(C):
        for m in range(1, C):
            plane_copy(i, m).wait_send()
        for n in range(1, G):
            group_copy(i, n).wait_send()


def grid_product(R, C, a, l, left):
    rows, cols = l.shape
    G = R // C
    depth = a.shape[1]
    vmem = pl.BlockSpec(memory_space=pltpu.VMEM)
    dma = pltpu.SemaphoreType.DMA
    return pl.pallas_call(
        functools.partial(product_kernel, R, C),
        out_shape=[
            jax.ShapeDtypeStruct((rows, cols), jnp.float32),
            jax.ShapeDtypeStruct((W // R, cols), jnp.float32),
        ],
        in_specs=[vmem, vmem, vmem],
        out_specs=[vmem, vmem],
        scratch_shapes=[
            pltpu.VMEM((C, rows // C, cols), jnp.float32),
            pltpu.VMEM((C, G, rows, cols), jnp.float32),
            pltpu.VMEM((C, rows, cols), jnp.float32),
            pltpu.VMEM((2, C // 2, rows, cols), jnp.float32),
            pltpu.VMEM((W, cols), jnp.float32),
            pltpu.VMEM((R - 1, W // R, cols), jnp.float32),
            pltpu.VMEM((rows, max(depth, W)), jnp.bfloat16),
            pltpu.VMEM((rows, max(depth, W)), jnp.bfloat16),
            pltpu.VMEM((max(depth, rows), cols), jnp.bfloat16),
            pltpu.VMEM((max(depth, rows), cols), jnp.bfloat16),
            dma((C - 1,)),
            dma((C - 1,)),
            dma((C - 1,)),
            dma((C - 1,)),
            dma((C, C - 1)),
            dma((C, C - 1)),
            dma((C, max(G - 1, 1))),
            dma((C, max(G - 1, 1))),
            dma((2, C // 2)),
            dma((2, C // 2)),
            dma((R - 1,)),
            dma((R - 1,)),
            dma((2,)),
        ],
        compiler_params=pltpu.CompilerParams(
            collective_id=0, has_side_effects=True, vmem_limit_bytes=67043328
        ),
    )(a, l, left)


def per_device(ancestor_inverse, factor, diag_inverse, widths, member):
    R = lax.axis_size("row")
    C = lax.axis_size("col")
    my_row = lax.axis_index("row")
    my_col = lax.axis_index("col")
    shard_cols = factor.shape[1]
    col_start = my_col * shard_cols
    global_cols = col_start + jnp.arange(shard_cols, dtype=jnp.int32)
    node_of = global_cols // W
    within = global_cols % W
    select = node_of[None, :] == jnp.arange(NODES, dtype=jnp.int32)[:, None]
    width_col = jnp.sum(jnp.where(select, widths[:, None], 0), axis=0)
    col_keep = within < width_col
    pick = jnp.where(select & col_keep[None, :], 1.0, 0.0).astype(jnp.bfloat16)
    mask = lax.dot_general(
        member.astype(jnp.bfloat16), pick, (((0,), (0,)), ((), ())),
        preferred_element_type=jnp.float32,
    )
    masked = factor * mask
    if shard_cols == W:
        left = masked
    else:
        rows_full = lax.all_gather(masked, "col", axis=1, tiled=True)
        left = lax.dynamic_slice_in_dim(rows_full, col_start // W * W, W, 1)
    product, gram = grid_product(R, C, ancestor_inverse, masked, left)
    offdiag = -product * mask
    diag_rows = diag_inverse.shape[0]
    local_rows = my_row * diag_rows + jnp.arange(diag_rows, dtype=jnp.int32)
    inside = (local_rows[:, None] < width_col[None, :]) & col_keep[None, :]
    diag_blocks = (diag_inverse + gram) * inside.astype(jnp.float32)
    return (offdiag, diag_blocks)


def solution(mesh):
    in_specs = (P("row", "col"), P("row", "col"), P("row", "col"), P(), P(None, "row"))
    out_specs = (P("row", "col"), P("row", "col"))
    return jax.shard_map(
        per_device, mesh=mesh, in_specs=in_specs, out_specs=out_specs, check_vma=False
    )
```
